32 devices in a mesh: blk: 4 (over y, x), strata: 8 (over z, core).
Axes of the slice: x: 2, y: 2, z: 4, core: 2. Of those that a mesh axis runs over, the one named last changes fastest.
Arguments:
- user_factors: bfloat16 [4096, 256], P('blk'), may hold values from -1.5 to 1.5
- item_factors: bfloat16 [8192, 256], P(('blk', 'strata')), may hold values from -1.5 to 1.5
- ratings: bfloat16 [4, 4, 8, 8, 128, 128], P('blk', None, 'strata'), may hold values from -6 to 6
- tile_user: int32 [4, 4, 8, 8], P('blk', None, 'strata'), may hold values from 0 to 7
- tile_item: int32 [4, 4, 8, 8], P('blk', None, 'strata'), may hold values from 0 to 1
- tile_count: int32 [4, 4, 8], P('blk', None, 'strata'), may hold values from 1 to 8, 40 in all within a row
Outputs:
- user_grad: float32 [4096, 256], P('blk')
- item_grad: float32 [8192, 256], P(('blk', 'strata'))
The draws below stay inside these ranges and needn't reach their ends.
Inputs may be any that keep to these rules, and one draw needn't show every extreme that they name: `tile_count`: for each user block and panel index, the counts over the strata are uneven and one of them equals 8.
All inputs are finite; a program needn't handle non-finite values.
Results may differ from the reference program's by a relative error of at most 0.0012.
Values may be sent and summed in bfloat16 or wider, within the bound.
A program may use at most 64 MiB of HBM per device.

```python
import math
import jax
import jax.numpy as jnp
import numpy as np
from jax import lax

R = 256
TILE = 128
TILES = 8
UT = 8
PT = 2
USERS = 4096
ITEMS = 8192
N_BLK = 4
N_STRATA = 8


def touch_ends(values, stream_key, low, top_value):
    shape = values.shape
    place = [jax.random.randint(jax.random.fold_in(stream_key, axis), (), 0, shape[axis]) for axis in range(len(shape))]
    values = values.at[tuple(place)].set(low)
    longest = shape.index(max(shape))
    place[longest] = (place[longest] + 1) % shape[longest]
    return values.at[tuple(place)].set(top_value)


def level_of(stream_key, dims, pieces, low, largest):
    loudness = 1.0
    for position, blocks in pieces:
        draws = jax.random.uniform(jax.random.fold_in(jax.random.fold_in(stream_key, 6), position), (blocks,), jnp.float32, low / len(pieces), largest / len(pieces))
        loudness = loudness * jnp.repeat(jnp.exp(draws), dims[position] // blocks).reshape((-1,) + (1,) * (len(dims) - 1 - position))
    return loudness


def profile(count, total, most, skew):
    loads = [(1 << 20) // math.isqrt(grade ** skew) + 1 for grade in range(2, count + 1)]
    surplus, counts = total - most - (count - 1), [1] * (count - 1)
    while surplus > 0:
        free = [i for i in range(count - 1) if counts[i] < most]
        whole, left = sum([loads[i] for i in free]), surplus
        for i in free:
            extra = min(most - counts[i], max(1, left * loads[i] // whole), surplus)
            counts[i] = counts[i] + extra
            surplus = surplus - extra
    return np.array([most] + counts)


def uneven_parts(key, number_of, total, bound, slope):
    if number_of == 2:
        one = jax.random.randint(key, (), max(1, total - bound), min(bound, total - 1) + 1)
        return jnp.stack([one, total - one])
    sizes = jnp.asarray(profile(number_of, total, bound, slope), jnp.int32)
    twos = (number_of - 1) // 2
    giver, receiver = sizes[1:1 + 2 * twos:2], sizes[2:2 + 2 * twos:2]
    margin = jnp.minimum(giver - 1, bound - receiver)
    moved = jax.random.randint(jax.random.fold_in(key, 1), (twos,), 0, 1 << 20) % (margin + 1)
    sizes = sizes.at[1:1 + 2 * twos:2].set(giver - moved).at[2:2 + 2 * twos:2].set(receiver + moved)
    return sizes[jax.random.permutation(jax.random.fold_in(key, 2), number_of)]


def noise(own_key, dims, deviation, limit, split=(), held_as=jnp.bfloat16):
    loudness = level_of(own_key, dims, split, -0.22, 0.18) if split else 1.0
    drawn = jax.random.normal(own_key, dims, jnp.float32) * deviation * loudness
    return jnp.minimum(jnp.maximum(drawn, -limit), limit).astype(held_as)


def setup_inputs(seed: int = 0) -> dict:
    streams_of = jax.random.split(jax.random.key(seed), 7)
    user_factors = noise(streams_of[0], (USERS, R), 0.25, 1.5, ((0, 4),))
    item_factors = noise(streams_of[1], (ITEMS, R), 0.25, 1.5, ((0, 32),))
    ratings = noise(streams_of[2], (N_BLK, N_BLK, N_STRATA, TILES, TILE, TILE), 1.0, 6.0, ((0, 4), (2, 8)))
    tile_user = touch_ends(jax.random.randint(streams_of[3], (N_BLK, N_BLK, N_STRATA, TILES), 0, UT), jax.random.fold_in(streams_of[3], 1), 0, UT - 1).astype(jnp.int32)
    tile_item = touch_ends(jax.random.randint(streams_of[4], (N_BLK, N_BLK, N_STRATA, TILES), 0, PT), jax.random.fold_in(streams_of[4], 1), 0, PT - 1).astype(jnp.int32)
    tile_count = jax.vmap(lambda own: uneven_parts(own, N_STRATA, N_STRATA * TILES * 5 // 8, TILES, 2))(jax.random.split(streams_of[5], N_BLK * N_BLK)).reshape((N_BLK, N_BLK, N_STRATA)).astype(jnp.int32)
    return {"user_factors": user_factors, "item_factors": item_factors, "ratings": ratings, "tile_user": tile_user, "tile_item": tile_item, "tile_count": tile_count}


def tile_terms(user_tiles, panel_tiles, rating_tiles, rows, cols, count):
    picked_users = jnp.take(user_tiles, rows, axis=0).astype(jnp.float32)
    picked_items = jnp.take(panel_tiles, cols, axis=0).astype(jnp.float32)
    predicted = jnp.einsum('kar,kbr->kab', picked_users, picked_items, precision=lax.Precision.HIGHEST)
    live = (jnp.arange(TILES) < count).astype(jnp.float32)
    residue = ((predicted - rating_tiles.astype(jnp.float32)) * live[:, None, None]).astype(jnp.bfloat16)
    wide = residue.astype(jnp.float32)
    user_part = jnp.einsum('kab,kbr->kar', wide, picked_items, precision=lax.Precision.HIGHEST) / TILE
    item_part = jnp.einsum('kab,kar->kbr', wide, picked_users, precision=lax.Precision.HIGHEST) / TILE
    user_hot = (rows[:, None] == jnp.arange(UT)[None, :]).astype(jnp.float32)
    item_hot = (cols[:, None] == jnp.arange(PT)[None, :]).astype(jnp.float32)
    user_sum = jnp.einsum('ku,kar->uar', user_hot, user_part, precision=lax.Precision.HIGHEST)
    item_sum = jnp.einsum('kp,kbr->pbr', item_hot, item_part, precision=lax.Precision.HIGHEST)
    return user_sum, item_sum


def reference(user_factors, item_factors, ratings, tile_user, tile_item, tile_count):
    users = user_factors.reshape(N_BLK, UT, TILE, R)
    items = item_factors.reshape(N_BLK, N_STRATA, PT, TILE, R)
    strata_terms = jax.vmap(tile_terms, in_axes=(None, 0, 0, 0, 0, 0))

    def visit(pair, carry):
        user_total, item_total = carry
        owner = pair // N_BLK
        source = pair % N_BLK
        user_parts, item_parts = strata_terms(users[owner], items[source], ratings[owner, source],
                                              tile_user[owner, source], tile_item[owner, source],
                                              tile_count[owner, source])
        user_total = user_total.at[owner].add(jnp.sum(user_parts, axis=0))
        item_total = item_total.at[source].add(item_parts)
        return user_total, item_total

    start = (jnp.zeros((N_BLK, UT, TILE, R), jnp.float32), jnp.zeros((N_BLK, N_STRATA, PT, TILE, R), jnp.float32))
    user_total, item_total = lax.fori_loop(0, N_BLK * N_BLK, visit, start)
    return user_total.reshape(USERS, R), item_total.reshape(ITEMS, R)
```

```python
import functools

import jax
import jax.numpy as jnp
from jax import lax
from jax.experimental import pallas as pl
from jax.experimental.pallas import tpu as pltpu
from jax.sharding import PartitionSpec as P

MESH = pl.DeviceIdType.MESH
F32 = jnp.float32
BF16 = jnp.bfloat16
CHUNK = 64
LAG = 4
STEP_LAG = 8
PARTS = 2


def flip(place, step, size):
    other, bit = 0, 1
    while bit < size:
        other = other + bit * ((place // bit + step // bit) % 2)
        bit *= 2
    return other


def encode(x):
    return (x * jnp.abs(x) * (x * x)).astype(BF16)


def decode(code):
    y = code.astype(F32)
    size = jnp.maximum(jnp.abs(y), 1e-37)
    root = lax.rsqrt(size)
    return y * root * lax.rsqrt(size * root)


def kernel(
    n_blk,
    n_strata,
    users_hbm,
    items_hbm,
    ratings_hbm,
    rows_hbm,
    cols_hbm,
    count_hbm,
    user_out,
    item_out,
    rows_ref,
    cols_ref,
    count_ref,
    user_table,
    panels,
    panel_table,
    ratings,
    picked_users,
    picked_items,
    residue,
    user_sum,
    pair_recv,
    side_send,
    side_recv,
    item_own,
    item_send,
    item_recv,
    load_sem,
    rating_sem,
    gather_recv,
    item_recv_sem,
    pair_recv_sem,
    side_recv_sem,
    share_recv_sem,
    send_sem,
):
    user_tiles, tile, rank = user_table.shape
    panel_tiles = panels.shape[1]
    panel_rows = panel_tiles * tile
    slots = ratings.shape[1]
    chunks = side_send.shape[1]
    per_tile = tile // CHUNK
    blk = lax.axis_index("blk")
    strata = lax.axis_index("strata")
    core = strata % 2
    sibling = strata + 1 - 2 * core
    chip = strata // 2
    chips = n_strata // 2
    half = chips // 2
    upper = chip // half
    sign = 1 - 2 * upper
    far = (chip + sign) * 2 + core
    near = (chip - sign) * 2 + core
    depth = chip + upper * (chips - 1 - 2 * chip)
    has_near = depth > 0
    lag = LAG + STEP_LAG * (half - 1 - depth)
    crossing = depth // (half - 1) if half > 1 else depth + 1
    square = n_blk == 4
    greeted = (1, 2) if square else tuple(range(1, n_blk))

    loads = [
        pltpu.make_async_copy(rows_hbm, rows_ref, load_sem.at[0]),
        pltpu.make_async_copy(cols_hbm, cols_ref, load_sem.at[1]),
        pltpu.make_async_copy(count_hbm, count_ref, load_sem.at[2]),
        pltpu.make_async_copy(items_hbm, panels.at[0], load_sem.at[3]),
        pltpu.make_async_copy(users_hbm, user_table, load_sem.at[4]),
    ]

    barrier = pltpu.get_barrier_semaphore()
    for step in greeted:
        pl.semaphore_signal(
            barrier, 1, device_id=(flip(blk, step, n_blk), strata), device_id_type=MESH
        )
    pl.semaphore_signal(barrier, 1, device_id=(blk, far), device_id_type=MESH)

    @pl.when(has_near)
    def _():
        pl.semaphore_signal(barrier, 1, device_id=(blk, near), device_id_type=MESH)

    pl.semaphore_signal(barrier, 1, device_id=(blk, sibling), device_id_type=MESH)

    for load in loads:
        load.start()

    def rating_copy(step):
        source = flip(blk, step, n_blk)
        return pltpu.make_async_copy(
            ratings_hbm.at[0, source, 0], ratings.at[step], rating_sem.at[step]
        )

    for step in range(n_blk):
        rating_copy(step).start()

    def remote(src, dst, send, recv, device):
        return pltpu.make_async_remote_copy(
            src_ref=src,
            dst_ref=dst,
            send_sem=send,
            recv_sem=recv,
            device_id=device,
            device_id_type=MESH,
        )

    def peer(step):
        return (flip(blk, step, n_blk), strata)

    part = tile // PARTS

    def direct_copy(step):
        return remote(
            panels.at[0], panels.at[step], send_sem.at[0], gather_recv.at[step], peer(step)
        )

    def first_copy(step, q):
        place = (step - 1, pl.ds(q * part, part))
        return remote(
            panels.at[(0,) + place], panels.at[(step,) + place],
            send_sem.at[0], gather_recv.at[(step - 1) * PARTS + q], peer(step),
        )

    def rest_copy(step):
        return remote(
            panels.at[0, 2 - step], panels.at[step, 2 - step],
            send_sem.at[0], gather_recv.at[2 * PARTS + step - 1], peer(step),
        )

    def forward_copy(step, q):
        place = (step - 1, pl.ds(q * part, part))
        return remote(
            panels.at[(step,) + place], panels.at[(3,) + place],
            send_sem.at[0], gather_recv.at[2 * PARTS + 2 + (step - 1) * PARTS + q],
            peer(3 - step),
        )

    def item_copy(step):
        return remote(
            item_send.at[step], item_recv.at[step],
            send_sem.at[1], item_recv_sem.at[step], peer(step),
        )

    def pair_copy(q):
        return remote(
            user_sum.at[pl.ds((2 * q + 1 - core) * tile, tile)],
            pair_recv.at[pl.ds(q * tile, tile)],
            send_sem.at[2], pair_recv_sem.at[q], (blk, sibling),
        )

    def far_copy(c):
        return remote(
            side_send.at[0, c], side_recv.at[crossing, c],
            send_sem.at[3], side_recv_sem.at[crossing, c], (blk, far),
        )

    def near_copy(c):
        return remote(
            side_send.at[1, c], side_recv.at[1, c],
            send_sem.at[4], side_recv_sem.at[1, c], (blk, near),
        )

    def arrived(side, c):
        return remote(
            side_send.at[0, c], side_recv.at[side, c],
            send_sem.at[3], side_recv_sem.at[side, c], (blk, far),
        )

    def own_rows(c, owner):
        return pl.ds((2 * (c // per_tile) + owner) * tile + (c % per_tile) * CHUNK, CHUNK)

    def share_copy(c, owner):
        return remote(
            user_out.at[own_rows(c, core)], user_out.at[own_rows(c, owner)],
            send_sem.at[5], share_recv_sem.at[c], (blk, sibling),
        )

    user_sum[...] = jnp.zeros(user_sum.shape, F32)

    def residues(step):
        source = flip(blk, step, n_blk)
        cols = [cols_ref[0, source, 0, k] for k in range(slots)]
        panel_table[...] = panels[step]
        for k in range(slots):
            place = slice(k * tile, (k + 1) * tile)
            picked_users[step, place] = user_table[rows_ref[0, source, 0, k]]
            picked_items[place] = panel_table[cols[k]]
        predicted = lax.dot_general(
            picked_users[step],
            panels[step].reshape(panel_rows, rank),
            (((1,), (1,)), ((), ())),
            preferred_element_type=F32,
        )
        for k in range(slots):
            place = slice(k * tile, (k + 1) * tile)
            live = (k < count_ref[0, 0, source]).astype(F32)
            chosen = predicted[place, :tile]
            for p in range(1, panel_tiles):
                chosen = jnp.where(cols[k] == p, predicted[place, p * tile : (p + 1) * tile], chosen)
            residue[step, place] = (
                (chosen - ratings[step, k].astype(F32)) * live
            ).astype(BF16)

    def hot(index, place):
        return jnp.full((tile, tile), (index == place).astype(F32), F32).astype(BF16)

    def user_terms(step):
        source = flip(blk, step, n_blk)

        def two_tiles(q, carry):
            rows = [
                jnp.concatenate(
                    [
                        residue[step, k * tile : (k + 1) * tile]
                        * hot(rows_ref[0, source, 0, k], 2 * q + one)
                        for k in range(slots)
                    ],
                    axis=1,
                )
                for one in range(2)
            ]
            place = pl.ds(2 * q * tile, 2 * tile)
            user_sum[place] += jnp.dot(
                jnp.concatenate(rows, axis=0), picked_items[...], preferred_element_type=F32
            )

            @pl.when(step == n_blk - 1)
            def _():
                pair_copy(q).start()

            return carry

        lax.fori_loop(0, user_tiles // 2, two_tiles, 0)

    def item_terms(step):
        source = flip(blk, step, n_blk)
        by_item = jnp.concatenate(
            [
                jnp.concatenate(
                    [
                        residue[step, k * tile : (k + 1) * tile]
                        * hot(cols_ref[0, source, 0, k], p)
                        for p in range(panel_tiles)
                    ],
                    axis=1,
                )
                for k in range(slots)
            ],
            axis=0,
        )
        return lax.dot_general(
            by_item,
            picked_users[step],
            (((0,), (0,)), ((), ())),
            preferred_element_type=F32,
        )

    for load in loads:
        load.wait()

    waits = 2 + len(greeted)

    @pl.when(has_near)
    def _():
        pl.semaphore_wait(barrier, waits + 1)

    @pl.when(depth == 0)
    def _():
        pl.semaphore_wait(barrier, waits)

    if square:
        for q in range(PARTS):
            for step in (1, 2):
                first_copy(step, q).start()
        for step in (1, 2):
            rest_copy(step).start()
    else:
        for step in range(1, n_blk):
            direct_copy(step).start()

    def visit(step, carry):
        @pl.when(step > 0)
        def _():
            if square:
                for one in (1, 2):
                    @pl.when(step == one)
                    def _():
                        rest_copy(one).wait_recv()

                @pl.when(step == 3)
                def _():
                    for one in (1, 2):
                        for q in range(PARTS):
                            forward_copy(one, q).wait_recv()
            else:
                direct_copy(step).wait_recv()

        rating_copy(step).wait()
        residues(step)
        user_terms(step)

        @pl.when(step == 0)
        def _():
            if square:
                for q in range(PARTS):
                    for one in (1, 2):
                        first_copy(one, q).wait_recv()
                        forward_copy(one, q).start()

        return carry

    lax.fori_loop(0, n_blk, visit, 0)

    def mine_at(c):
        return pair_recv.at[pl.ds(c * CHUNK, CHUNK)]

    def fold(c, carry):
        @pl.when(c % per_tile == 0)
        def _():
            pair_copy(c // per_tile).wait_recv()

        mine = mine_at(c)
        mine[...] += user_sum[own_rows(c, core)]

        @pl.when(depth == 0)
        def _():
            side_send[0, c] = encode(mine[...])
            far_copy(c).start()

        return carry

    lax.fori_loop(0, chunks, fold, 0)

    def return_items(step, carry):
        terms = item_terms(step)

        @pl.when(step == 0)
        def _():
            item_own[...] = terms

        @pl.when(step > 0)
        def _():
            item_send[step] = encode(terms)
            item_copy(step).start()

        return carry

    lax.fori_loop(0, n_blk, return_items, 0)

    def hop(t, carry):
        @pl.when((t < chunks) & has_near)
        def _():
            arrived(0, t).wait_recv()
            mine = mine_at(t)
            total = mine[...] + decode(side_recv[0, t])
            user_out[own_rows(t, core)] = total
            side_send[0, t] = encode(total)
            far_copy(t).start()

        @pl.when(t >= lag)
        def _():
            c = t - lag
            arrived(1, c).wait_recv()
            beyond = decode(side_recv[1, c])
            mine = mine_at(c)

            @pl.when(has_near)
            def _():
                side_send[1, c] = encode(mine[...] + beyond)
                near_copy(c).start()
                user_out[own_rows(c, core)] = (user_out[own_rows(c, core)] + beyond) * (1.0 / tile)

            @pl.when(depth == 0)
            def _():
                user_out[own_rows(c, core)] = (mine[...] + beyond) * (1.0 / tile)

            share_copy(c, core).start()

        return carry

    lax.fori_loop(0, chunks + lag, hop, 0)

    def settle(step, carry):
        item_copy(step).wait_recv()
        item_own[...] += decode(item_recv[step])
        return carry

    lax.fori_loop(1, n_blk, settle, 0)
    item_out[...] = item_own[...] * (1.0 / tile)

    def drain(ref, which):
        remote(ref, ref, send_sem.at[which], share_recv_sem.at[0], (blk, sibling)).wait_send()

    drain(panels.at[pl.ds(1, n_blk - 1)], 0)
    drain(item_send.at[pl.ds(1, n_blk - 1)], 1)
    drain(pair_recv, 2)
    drain(side_send.at[0], 3)

    @pl.when(has_near)
    def _():
        drain(side_send.at[1], 4)

    drain(pair_recv, 5)

    def drain_chunks(c, carry):
        share_copy(c, 1 - core).wait_recv()
        return carry

    lax.fori_loop(0, chunks, drain_chunks, 0)


def body(user_factors, item_factors, ratings, tile_user, tile_item, tile_count):
    n_blk = lax.axis_size("blk")
    n_strata = lax.axis_size("strata")
    user_rows, rank = user_factors.shape
    panel_rows = item_factors.shape[0]
    slots, tile = ratings.shape[-3], ratings.shape[-1]
    user_tiles, panel_tiles = user_rows // tile, panel_rows // tile
    chunks = user_rows // 2 // CHUNK
    dma = pltpu.SemaphoreType.DMA
    counts = jnp.swapaxes(tile_count, 1, 2)
    operands = (
        user_factors.reshape(user_tiles, tile, rank),
        item_factors.reshape(panel_tiles, tile, rank),
        ratings,
        tile_user,
        tile_item,
        counts,
    )
    return pl.pallas_call(
        functools.partial(kernel, n_blk, n_strata),
        out_shape=(
            jax.ShapeDtypeStruct((user_rows, rank), F32),
            jax.ShapeDtypeStruct((panel_rows, rank), F32),
        ),
        in_specs=[pl.BlockSpec(memory_space=pltpu.HBM)] * 6,
        out_specs=(
            pl.BlockSpec(memory_space=pltpu.VMEM),
            pl.BlockSpec(memory_space=pltpu.VMEM),
        ),
        scratch_shapes=[
            pltpu.SMEM(tile_user.shape, jnp.int32),
            pltpu.SMEM(tile_item.shape, jnp.int32),
            pltpu.SMEM(counts.shape, jnp.int32),
            pltpu.VMEM((user_tiles, tile, rank), BF16),
            pltpu.VMEM((n_blk, panel_tiles, tile, rank), BF16),
            pltpu.VMEM((panel_tiles, tile, rank), BF16),
            pltpu.VMEM((n_blk, slots, tile, tile), BF16),
            pltpu.VMEM((n_blk, slots * tile, rank), BF16),
            pltpu.VMEM((slots * tile, rank), BF16),
            pltpu.VMEM((n_blk, slots * tile, tile), BF16),
            pltpu.VMEM((user_rows, rank), F32),
            pltpu.VMEM((user_rows // 2, rank), F32),
            pltpu.VMEM((2, chunks, CHUNK, rank), BF16),
            pltpu.VMEM((2, chunks, CHUNK, rank), BF16),
            pltpu.VMEM((panel_rows, rank), F32),
            pltpu.VMEM((n_blk, panel_rows, rank), BF16),
            pltpu.VMEM((n_blk, panel_rows, rank), BF16),
            dma((5,)),
            dma((n_blk,)),
            dma((4 * PARTS + 2 if n_blk == 4 else n_blk,)),
            dma((n_blk,)),
            dma((user_tiles // 2,)),
            dma((2, chunks)),
            dma((chunks,)),
            dma((6,)),
        ],
        compiler_params=pltpu.CompilerParams(
            collective_id=0, has_side_effects=True, vmem_limit_bytes=48 << 20
        ),
    )(*(pltpu.with_memory_space_constraint(x, pltpu.HBM) for x in operands))


def solution(mesh):
    in_specs = (
        P("blk", None),
        P(("blk", "strata"), None),
        P("blk", None, "strata", None, None, None),
        P("blk", None, "strata", None),
        P("blk", None, "strata", None),
        P("blk", None, "strata"),
    )
    out_specs = (P("blk", None), P(("blk", "strata"), None))
    return jax.shard_map(body, mesh=mesh, in_specs=in_specs, out_specs=out_specs, check_vma=False)
```

```python
import functools

import jax
import jax.numpy as jnp
from jax import lax
from jax.experimental import pallas as pl
from jax.experimental.pallas import tpu as pltpu
from jax.sharding import PartitionSpec as P

MESH = pl.DeviceIdType.MESH
F32 = jnp.float32
BF16 = jnp.bfloat16
CHUNK = 32
LAG = 8
STEP_LAG = 16
TAIL = 4
PARTS = 2


def flip(place, step, size):
    other, bit = 0, 1
    while bit < size:
        other = other + bit * ((place // bit + step // bit) % 2)
        bit *= 2
    return other


def encode(x):
    return (x * jnp.abs(x) * (x * x)).astype(BF16)


def decode(code):
    y = code.astype(F32)
    size = jnp.maximum(jnp.abs(y), 1e-37)
    root = lax.rsqrt(size)
    return y * root * lax.rsqrt(size * root)


def kernel(
    n_blk,
    n_strata,
    users_hbm,
    items_hbm,
    ratings_hbm,
    rows_hbm,
    cols_hbm,
    count_hbm,
    user_out,
    item_out,
    rows_ref,
    cols_ref,
    count_ref,
    user_table,
    panels,
    panel_table,
    ratings,
    picked_users,
    picked_items,
    residue,
    user_sum,
    pair_recv,
    side_send,
    side_recv,
    item_own,
    item_send,
    item_recv,
    load_sem,
    rating_sem,
    gather_recv,
    item_recv_sem,
    pair_recv_sem,
    side_recv_sem,
    share_recv_sem,
    send_sem,
):
    user_tiles, tile, rank = user_table.shape
    panel_tiles = panels.shape[1]
    panel_rows = panel_tiles * tile
    slots = ratings.shape[1]
    chunks = side_send.shape[1]
    per_tile = tile // CHUNK
    blk = lax.axis_index("blk")
    strata = lax.axis_index("strata")
    core = strata % 2
    sibling = strata + 1 - 2 * core
    chip = strata // 2
    chips = n_strata // 2
    half = chips // 2
    upper = chip // half
    sign = 1 - 2 * upper
    far = (chip + sign) * 2 + core
    near = (chip - sign) * 2 + core
    depth = chip + upper * (chips - 1 - 2 * chip)
    has_near = depth > 0
    lag = LAG + STEP_LAG * (half - 1 - depth)
    crossing = depth // (half - 1) if half > 1 else depth + 1
    square = n_blk == 4
    tail = chunks - (TAIL * (1 - core) if half == 2 else 0)
    across = (chip + 2 * sign) * 2 + core
    greeted = (1, 2) if square else tuple(range(1, n_blk))

    loads = [
        pltpu.make_async_copy(rows_hbm, rows_ref, load_sem.at[0]),
        pltpu.make_async_copy(cols_hbm, cols_ref, load_sem.at[1]),
        pltpu.make_async_copy(count_hbm, count_ref, load_sem.at[2]),
        pltpu.make_async_copy(items_hbm, panels.at[0], load_sem.at[3]),
        pltpu.make_async_copy(users_hbm, user_table, load_sem.at[4]),
    ]

    barrier = pltpu.get_barrier_semaphore()
    for step in greeted:
        pl.semaphore_signal(
            barrier, 1, device_id=(flip(blk, step, n_blk), strata), device_id_type=MESH
        )
    pl.semaphore_signal(barrier, 1, device_id=(blk, far), device_id_type=MESH)

    @pl.when(has_near)
    def _():
        pl.semaphore_signal(barrier, 1, device_id=(blk, near), device_id_type=MESH)

    pl.semaphore_signal(barrier, 1, device_id=(blk, sibling), device_id_type=MESH)

    for load in loads:
        load.start()

    def rating_copy(step):
        source = flip(blk, step, n_blk)
        return pltpu.make_async_copy(
            ratings_hbm.at[0, source, 0], ratings.at[step], rating_sem.at[step]
        )

    for step in range(n_blk):
        rating_copy(step).start()

    def remote(src, dst, send, recv, device):
        return pltpu.make_async_remote_copy(
            src_ref=src,
            dst_ref=dst,
            send_sem=send,
            recv_sem=recv,
            device_id=device,
            device_id_type=MESH,
        )

    def peer(step):
        return (flip(blk, step, n_blk), strata)

    part = tile // PARTS

    def direct_copy(step):
        return remote(
            panels.at[0], panels.at[step],
            send_sem.at[0], gather_recv.at[2 * PARTS + 2 if square else step], peer(step),
        )

    def first_copy(step, q):
        place = (step - 1, pl.ds(q * part, part))
        return remote(
            panels.at[(0,) + place], panels.at[(step,) + place],
            send_sem.at[0], gather_recv.at[(step - 1) * PARTS + q], peer(step),
        )

    def rest_copy(step):
        return remote(
            panels.at[0, 2 - step], panels.at[step, 2 - step],
            send_sem.at[0], gather_recv.at[2 * PARTS + step - 1], peer(step),
        )

    def forward_copy(step, q):
        place = (step - 1, pl.ds(q * part, part))
        return remote(
            panels.at[(step,) + place], panels.at[(3,) + place],
            send_sem.at[0], gather_recv.at[2 * PARTS + 2],
            peer(3 - step),
        )

    def item_copy(step):
        return remote(
            item_send.at[step], item_recv.at[step],
            send_sem.at[1], item_recv_sem.at[step - 1], peer(step),
        )

    def pair_copy(q):
        return remote(
            user_sum.at[pl.ds((2 * q + 1 - core) * tile, tile)],
            pair_recv.at[pl.ds(q * tile, tile)],
            send_sem.at[2], pair_recv_sem.at[q], (blk, sibling),
        )

    def far_copy(c):
        return remote(
            side_send.at[0, c], side_recv.at[crossing, c],
            send_sem.at[3], side_recv_sem.at[crossing, c], (blk, far),
        )

    def near_copy(c):
        return remote(
            side_send.at[1, c], side_recv.at[1, c],
            send_sem.at[4], side_recv_sem.at[1, c], (blk, near),
        )

    def ahead_copy(c):
        return remote(
            side_send.at[1, c], side_recv.at[0, c],
            send_sem.at[4], side_recv_sem.at[0, c], (blk, near),
        )

    def across_copy(c):
        return remote(
            side_send.at[0, c], side_recv.at[1, c],
            send_sem.at[6], side_recv_sem.at[1, c], (blk, across),
        )

    def arrived(side, c):
        return remote(
            side_send.at[0, c], side_recv.at[side, c],
            send_sem.at[3], side_recv_sem.at[side, c], (blk, far),
        )

    def own_rows(c, owner):
        return pl.ds((2 * (c // per_tile) + owner) * tile + (c % per_tile) * CHUNK, CHUNK)

    def share_copy(c):
        return remote(
            user_out.at[own_rows(c, core)], user_out.at[own_rows(c, core)],
            send_sem.at[5], share_recv_sem.at[0], (blk, sibling),
        )

    user_sum[...] = jnp.zeros(user_sum.shape, F32)

    def residues(step):
        source = flip(blk, step, n_blk)
        cols = [cols_ref[0, source, 0, k] for k in range(slots)]
        panel_table[...] = panels[step]
        for k in range(slots):
            place = slice(k * tile, (k + 1) * tile)
            picked_users[step, place] = user_table[rows_ref[0, source, 0, k]]
            picked_items[place] = panel_table[cols[k]]
        predicted = lax.dot_general(
            picked_users[step],
            panels[step].reshape(panel_rows, rank),
            (((1,), (1,)), ((), ())),
            preferred_element_type=F32,
        )
        for k in range(slots):
            place = slice(k * tile, (k + 1) * tile)
            live = (k < count_ref[0, 0, source]).astype(F32)
            chosen = predicted[place, :tile]
            for p in range(1, panel_tiles):
                chosen = jnp.where(cols[k] == p, predicted[place, p * tile : (p + 1) * tile], chosen)
            residue[step, place] = (
                (chosen - ratings[step, k].astype(F32)) * live
            ).astype(BF16)

    def hot(index, place):
        return jnp.full((tile, tile), (index == place).astype(F32), F32).astype(BF16)

    def mine_at(c):
        return pair_recv.at[pl.ds(c * CHUNK, CHUNK)]

    def fold(c, carry):
        @pl.when(c % per_tile == 0)
        def _():
            pair_copy(c // per_tile).wait_recv()

        mine = mine_at(c)
        mine[...] += user_sum[own_rows(c, core)]

        @pl.when(depth == 0)
        def _():
            side_send[0, c] = encode(mine[...])
            far_copy(c).start()

        @pl.when(has_near & (c >= tail))
        def _():
            side_send[1, c] = encode(mine[...])
            ahead_copy(c).start()

        return carry

    def user_terms(step, last):
        source = flip(blk, step, n_blk)
        for q in range(user_tiles // 2):
            rows = [
                jnp.concatenate(
                    [
                        residue[step, k * tile : (k + 1) * tile]
                        * hot(rows_ref[0, source, 0, k], 2 * q + one)
                        for k in range(slots)
                    ],
                    axis=1,
                )
                for one in range(2)
            ]
            place = slice(2 * q * tile, 2 * (q + 1) * tile)
            user_sum[place] += jnp.dot(
                jnp.concatenate(rows, axis=0), picked_items[...], preferred_element_type=F32
            )
            if last:
                pair_copy(q).start()

                @pl.when(core == 0)
                def _():
                    lax.fori_loop(q * per_tile, (q + 1) * per_tile, fold, 0)

    def item_terms(step):
        source = flip(blk, step, n_blk)
        by_item = jnp.concatenate(
            [
                jnp.concatenate(
                    [
                        residue[step, k * tile : (k + 1) * tile]
                        * hot(cols_ref[0, source, 0, k], p)
                        for p in range(panel_tiles)
                    ],
                    axis=1,
                )
                for k in range(slots)
            ],
            axis=0,
        )
        return lax.dot_general(
            by_item,
            picked_users[step],
            (((0,), (0,)), ((), ())),
            preferred_element_type=F32,
        )

    for load in loads:
        load.wait()

    waits = 2 + len(greeted)

    @pl.when(has_near)
    def _():
        pl.semaphore_wait(barrier, waits + 1)

    @pl.when(depth == 0)
    def _():
        pl.semaphore_wait(barrier, waits)

    if square:
        for q in range(PARTS):
            for step in (1, 2):
                first_copy(step, q).start()
        for step in (1, 2):
            rest_copy(step).start()
    else:
        for step in range(1, n_blk):
            direct_copy(step).start()

    def visit(step, carry):
        if square:
            for one in (1, 2):
                @pl.when(step == one)
                def _():
                    rest_copy(one).wait_recv()
        else:
            @pl.when(step > 0)
            def _():
                direct_copy(step).wait_recv()

        rating_copy(step).wait()
        residues(step)
        user_terms(step, False)

        if square:
            @pl.when(step == 0)
            def _():
                for q in range(PARTS):
                    for one in (1, 2):
                        first_copy(one, q).wait_recv()
                        forward_copy(one, q).start()

        return carry

    final = n_blk - 1
    lax.fori_loop(0, final, visit, 0)
    direct_copy(final).wait_recv()
    rating_copy(final).wait()
    residues(final)
    user_terms(final, True)

    @pl.when(core == 1)
    def _():
        lax.fori_loop(0, chunks, fold, 0)

    def return_items(step, carry):
        terms = item_terms(step)

        @pl.when(step == 0)
        def _():
            item_own[...] = terms

        @pl.when(step > 0)
        def _():
            item_send[step] = encode(terms)
            item_copy(step).start()

        return carry

    lax.fori_loop(0, n_blk, return_items, 0)

    def hop(t, carry):
        @pl.when((t < chunks) & has_near)
        def _():
            arrived(0, t).wait_recv()
            total = mine_at(t)[...] + decode(side_recv[0, t])
            user_out[own_rows(t, core)] = total
            side_send[0, t] = encode(total)

            @pl.when(t >= tail)
            def _():
                across_copy(t).start()

            far_copy(t).start()

        @pl.when(t >= lag)
        def _():
            c = t - lag
            mine = mine_at(c)

            @pl.when((depth == 0) & (c < tail))
            def _():
                user_out[own_rows(c, core)] = mine[...]

            @pl.when((depth == 0) & (c >= tail))
            def _():
                arrived(0, c).wait_recv()
                user_out[own_rows(c, core)] = mine[...] + decode(side_recv[0, c])

            arrived(1, c).wait_recv()
            beyond = decode(side_recv[1, c])

            @pl.when(has_near & (c < tail))
            def _():
                side_send[1, c] = encode(mine[...] + beyond)
                near_copy(c).start()

            user_out[own_rows(c, core)] = (user_out[own_rows(c, core)] + beyond) * (1.0 / tile)
            share_copy(c).start()

        return carry

    lax.fori_loop(0, chunks + lag, hop, 0)

    def settle(step, carry):
        item_copy(step).wait_recv()
        item_own[...] += decode(item_recv[step])
        return carry

    lax.fori_loop(1, n_blk, settle, 0)
    item_out[...] = item_own[...] * (1.0 / tile)

    def drain(ref, which):
        remote(ref, ref, send_sem.at[which], share_recv_sem.at[0], (blk, sibling)).wait_send()

    drain(panels.at[pl.ds(1, n_blk - 1)], 0)
    drain(item_send.at[pl.ds(1, n_blk - 1)], 1)
    drain(pair_recv, 2)
    drain(side_send.at[0], 3)

    @pl.when(has_near)
    def _():
        drain(side_send.at[1], 4)

    if half == 2:
        @pl.when(has_near & (core == 0))
        def _():
            drain(side_send.at[0, pl.ds(chunks - TAIL, TAIL)], 6)

    drain(pair_recv, 5)
    remote(
        pair_recv, pair_recv, send_sem.at[5], share_recv_sem.at[0], (blk, sibling)
    ).wait_recv()


def settle_out(user_ref, item_ref, user_out, item_out, sem):
    copies = (
        pltpu.make_async_copy(user_ref, user_out, sem.at[0]),
        pltpu.make_async_copy(item_ref, item_out, sem.at[1]),
    )
    for copy in copies:
        copy.start()
    for copy in copies:
        copy.wait()


def body(user_factors, item_factors, ratings, tile_user, tile_item, tile_count):
    n_blk = lax.axis_size("blk")
    n_strata = lax.axis_size("strata")
    user_rows, rank = user_factors.shape
    panel_rows = item_factors.shape[0]
    slots, tile = ratings.shape[-3], ratings.shape[-1]
    user_tiles, panel_tiles = user_rows // tile, panel_rows // tile
    chunks = user_rows // 2 // CHUNK
    dma = pltpu.SemaphoreType.DMA
    counts = jnp.swapaxes(tile_count, 1, 2)
    operands = (
        user_factors.reshape(user_tiles, tile, rank),
        item_factors.reshape(panel_tiles, tile, rank),
        ratings,
        tile_user,
        tile_item,
        counts,
    )
    shapes = (
        jax.ShapeDtypeStruct((user_rows, rank), F32),
        jax.ShapeDtypeStruct((panel_rows, rank), F32),
    )
    grads = pl.pallas_call(
        functools.partial(kernel, n_blk, n_strata),
        out_shape=shapes,
        in_specs=[pl.BlockSpec(memory_space=pltpu.HBM)] * 6,
        out_specs=(
            pl.BlockSpec(memory_space=pltpu.VMEM),
            pl.BlockSpec(memory_space=pltpu.VMEM),
        ),
        scratch_shapes=[
            pltpu.SMEM(tile_user.shape, jnp.int32),
            pltpu.SMEM(tile_item.shape, jnp.int32),
            pltpu.SMEM(counts.shape, jnp.int32),
            pltpu.VMEM((user_tiles, tile, rank), BF16),
            pltpu.VMEM((n_blk, panel_tiles, tile, rank), BF16),
            pltpu.VMEM((panel_tiles, tile, rank), BF16),
            pltpu.VMEM((n_blk, slots, tile, tile), BF16),
            pltpu.VMEM((n_blk, slots * tile, rank), BF16),
            pltpu.VMEM((slots * tile, rank), BF16),
            pltpu.VMEM((n_blk, slots * tile, tile), BF16),
            pltpu.VMEM((user_rows, rank), F32),
            pltpu.VMEM((user_rows // 2, rank), F32),
            pltpu.VMEM((2, chunks, CHUNK, rank), BF16),
            pltpu.VMEM((2, chunks, CHUNK, rank), BF16),
            pltpu.VMEM((panel_rows, rank), F32),
            pltpu.VMEM((n_blk, panel_rows, rank), BF16),
            pltpu.VMEM((n_blk, panel_rows, rank), BF16),
            dma((5,)),
            dma((n_blk,)),
            dma((2 * PARTS + 3 if n_blk == 4 else n_blk,)),
            dma((n_blk - 1,)),
            dma((user_tiles // 2,)),
            dma((2, chunks)),
            dma((1,)),
            dma((7,)),
        ],
        compiler_params=pltpu.CompilerParams(
            collective_id=0, has_side_effects=True, vmem_limit_bytes=48 << 20
        ),
    )(*(pltpu.with_memory_space_constraint(x, pltpu.HBM) for x in operands))
    return pl.pallas_call(
        settle_out,
        out_shape=shapes,
        in_specs=[pl.BlockSpec(memory_space=pl.ANY)] * 2,
        out_specs=(pl.BlockSpec(memory_space=pltpu.HBM),) * 2,
        scratch_shapes=[dma((2,))],
        compiler_params=pltpu.CompilerParams(vmem_limit_bytes=1 << 20),
        cost_estimate=pl.CostEstimate(
            flops=0, bytes_accessed=8 * (user_rows + panel_rows) * rank, transcendentals=0
        ),
    )(*grads)


def solution(mesh):
    in_specs = (
        P("blk", None),
        P(("blk", "strata"), None),
        P("blk", None, "strata", None, None, None),
        P("blk", None, "strata", None),
        P("blk", None, "strata", None),
        P("blk", None, "strata"),
    )
    out_specs = (P("blk", None), P(("blk", "strata"), None))
    return jax.shard_map(body, mesh=mesh, in_specs=in_specs, out_specs=out_specs, check_vma=False)
```

```python
import functools

import jax
import jax.numpy as jnp
from jax import lax
from jax.experimental import pallas as pl
from jax.experimental.pallas import tpu as pltpu
from jax.sharding import PartitionSpec as P

MESH = pl.DeviceIdType.MESH
F32 = jnp.float32
BF16 = jnp.bfloat16
CHUNK = 64
LAG = 8
STEP_LAG = 14
PARTS = 2


def flip(place, step, size):
    other, bit = 0, 1
    while bit < size:
        other = other + bit * ((place // bit + step // bit) % 2)
        bit *= 2
    return other


def encode(x):
    return (x * jnp.abs(x) * (x * x)).astype(BF16)


def decode(code):
    y = code.astype(F32)
    size = jnp.maximum(jnp.abs(y), 1e-37)
    root = lax.rsqrt(size)
    return y * root * lax.rsqrt(size * root)


def kernel(
    n_blk,
    n_strata,
    users_hbm,
    items_hbm,
    ratings_hbm,
    rows_hbm,
    cols_hbm,
    count_hbm,
    user_out,
    item_out,
    rows_ref,
    cols_ref,
    count_ref,
    user_table,
    panels,
    panel_table,
    ratings,
    picked_users,
    picked_items,
    residue,
    user_sum,
    pair_recv,
    side_send,
    side_recv,
    item_own,
    item_send,
    item_recv,
    load_sem,
    gather_recv,
    item_recv_sem,
    pair_recv_sem,
    side_recv_sem,
    share_recv_sem,
    send_sem,
):
    user_tiles, tile, rank = user_table.shape
    panel_tiles = panels.shape[1]
    panel_rows = panel_tiles * tile
    slots = ratings.shape[1]
    chunks = side_send.shape[1]
    per_tile = tile // CHUNK
    blk = lax.axis_index("blk")
    strata = lax.axis_index("strata")
    core = strata % 2
    sibling = strata + 1 - 2 * core
    chip = strata // 2
    chips = n_strata // 2
    half = chips // 2
    upper = chip // half
    sign = 1 - 2 * upper
    far = (chip + sign) * 2 + 1
    depth = chip + upper * (chips - 1 - 2 * chip)
    has_near = depth > 0
    inner = has_near & (core == 1)
    outer = depth == 0
    early_tiles = user_tiles // 4
    early = early_tiles * per_tile
    inner0 = (has_near & (core == 0)) | (outer & (core == 1))
    low = (1 - has_near.astype(jnp.int32)) * core * early
    high = core * chunks + (1 - core) * (1 - has_near.astype(jnp.int32)) * early
    lag = LAG + STEP_LAG * (half - 1 - depth)
    crossing = depth // (half - 1) if half > 1 else depth + 1
    square = n_blk == 4
    greeted = (1, 2) if square else tuple(range(1, n_blk))

    def near(c):
        kept = (depth == 1) & (c < early)
        return (chip - sign) * 2 + 1 - kept.astype(jnp.int32)

    loads = [
        pltpu.make_async_copy(rows_hbm, rows_ref, load_sem.at[0]),
        pltpu.make_async_copy(cols_hbm, cols_ref, load_sem.at[1]),
        pltpu.make_async_copy(count_hbm, count_ref, load_sem.at[2]),
        pltpu.make_async_copy(items_hbm, panels.at[0], load_sem.at[3]),
        pltpu.make_async_copy(users_hbm, user_table, load_sem.at[4]),
    ]

    barrier = pltpu.get_barrier_semaphore()
    for step in greeted:
        pl.semaphore_signal(
            barrier, 1, device_id=(flip(blk, step, n_blk), strata), device_id_type=MESH
        )

    @pl.when(outer | (core == 1))
    def _():
        pl.semaphore_signal(barrier, 1, device_id=(blk, far), device_id_type=MESH)

    @pl.when(inner)
    def _():
        pl.semaphore_signal(barrier, 1, device_id=(blk, near(chunks)), device_id_type=MESH)

    @pl.when(inner & (depth == 1))
    def _():
        pl.semaphore_signal(barrier, 1, device_id=(blk, near(0)), device_id_type=MESH)

    pl.semaphore_signal(barrier, 1, device_id=(blk, sibling), device_id_type=MESH)

    for load in loads:
        load.start()

    load_ratings = pltpu.make_async_copy(
        ratings_hbm.at[0, pl.ds(0, n_blk), 0], ratings, load_sem.at[5]
    )
    load_ratings.start()

    def remote(src, dst, send, recv, device):
        return pltpu.make_async_remote_copy(
            src_ref=src,
            dst_ref=dst,
            send_sem=send,
            recv_sem=recv,
            device_id=device,
            device_id_type=MESH,
        )

    def peer(step):
        return (flip(blk, step, n_blk), strata)

    part = tile // PARTS

    def direct_copy(step):
        return remote(
            panels.at[0], panels.at[step],
            send_sem.at[0], gather_recv.at[2 * PARTS + 2 if square else step], peer(step),
        )

    def first_copy(step, q):
        place = (step - 1, pl.ds(q * part, part))
        return remote(
            panels.at[(0,) + place], panels.at[(step,) + place],
            send_sem.at[0], gather_recv.at[(step - 1) * PARTS + q], peer(step),
        )

    def rest_copy(step):
        return remote(
            panels.at[0, 2 - step], panels.at[step, 2 - step],
            send_sem.at[0], gather_recv.at[2 * PARTS + step - 1], peer(step),
        )

    def forward_copy(step, q):
        place = (step - 1, pl.ds(q * part, part))
        return remote(
            panels.at[(step,) + place], panels.at[(3,) + place],
            send_sem.at[0], gather_recv.at[2 * PARTS + 2],
            peer(3 - step),
        )

    def item_copy(step):
        return remote(
            item_send.at[step], item_recv.at[step],
            send_sem.at[1], item_recv_sem.at[0], peer(step),
        )

    def pair_copy(u):
        place = pl.ds(u * tile, tile)
        return remote(
            user_sum.at[place], pair_recv.at[place],
            send_sem.at[2], pair_recv_sem.at[u], (blk, sibling),
        )

    def far_copy(c):
        return remote(
            side_send.at[0, c], side_recv.at[crossing, c],
            send_sem.at[3], side_recv_sem.at[crossing, c], (blk, far),
        )

    def near_copy(c):
        return remote(
            side_send.at[1, c], side_recv.at[1, c],
            send_sem.at[4], side_recv_sem.at[1, c], (blk, near(c)),
        )

    def arrived(side, c):
        return remote(
            side_send.at[0, c], side_recv.at[side, c],
            send_sem.at[3], side_recv_sem.at[side, c], (blk, far),
        )

    def rows_of(c):
        return pl.ds(c * CHUNK, CHUNK)

    def share_copy(c):
        return remote(
            user_out.at[rows_of(c)], user_out.at[rows_of(c)],
            send_sem.at[5], share_recv_sem.at[0], (blk, sibling),
        )

    user_sum[...] = jnp.zeros(user_sum.shape, F32)

    def residues(step):
        source = flip(blk, step, n_blk)
        cols = [cols_ref[0, source, 0, k] for k in range(slots)]
        panel_table[...] = panels[step]
        for k in range(slots):
            place = slice(k * tile, (k + 1) * tile)
            picked_users[step, place] = user_table[rows_ref[0, source, 0, k]]
            picked_items[place] = panel_table[cols[k]]
        predicted = lax.dot_general(
            picked_users[step],
            panels[step].reshape(panel_rows, rank),
            (((1,), (1,)), ((), ())),
            preferred_element_type=F32,
        )
        for k in range(slots):
            place = slice(k * tile, (k + 1) * tile)
            live = (k < count_ref[0, 0, source]).astype(F32)
            chosen = predicted[place, :tile]
            for p in range(1, panel_tiles):
                chosen = jnp.where(cols[k] == p, predicted[place, p * tile : (p + 1) * tile], chosen)
            residue[step, place] = (
                (chosen - ratings[source, k].astype(F32)) * live
            ).astype(BF16)

    def hot(index, place):
        return jnp.full((tile, tile), (index == place).astype(F32), F32).astype(BF16)

    def fold(c, carry):
        @pl.when(c % per_tile == 0)
        def _():
            pair_copy(c // per_tile).wait_recv()

        mine = user_sum[rows_of(c)] + pair_recv[rows_of(c)]
        user_sum[rows_of(c)] = mine

        @pl.when(depth == 0)
        def _():
            side_send[0, c] = encode(mine)
            far_copy(c).start()

        return carry

    def user_terms(step, last):
        source = flip(blk, step, n_blk)
        for q in range(user_tiles // 2):
            rows = [
                jnp.concatenate(
                    [
                        residue[step, k * tile : (k + 1) * tile]
                        * hot(rows_ref[0, source, 0, k], 2 * q + one)
                        for k in range(slots)
                    ],
                    axis=1,
                )
                for one in range(2)
            ]
            place = slice(2 * q * tile, 2 * (q + 1) * tile)
            user_sum[place] += jnp.dot(
                jnp.concatenate(rows, axis=0), picked_items[...], preferred_element_type=F32
            )
            if last:
                for u in (2 * q, 2 * q + 1):
                    away = inner0 if u < early_tiles else core == 0

                    @pl.when(away)
                    def _():
                        pair_copy(u).start()

                if 2 * q < early_tiles:
                    @pl.when(outer & (core == 0))
                    def _():
                        lax.fori_loop(2 * q * per_tile, 2 * (q + 1) * per_tile, fold, 0)

    def item_terms(step):
        source = flip(blk, step, n_blk)
        by_item = jnp.concatenate(
            [
                jnp.concatenate(
                    [
                        residue[step, k * tile : (k + 1) * tile]
                        * hot(cols_ref[0, source, 0, k], p)
                        for p in range(panel_tiles)
                    ],
                    axis=1,
                )
                for k in range(slots)
            ],
            axis=0,
        )
        return lax.dot_general(
            by_item,
            picked_users[step],
            (((0,), (0,)), ((), ())),
            preferred_element_type=F32,
        )

    for load in loads:
        load.wait()

    waits = 1 + len(greeted)

    @pl.when(has_near & (core == 0))
    def _():
        pl.semaphore_wait(barrier, waits)

    @pl.when(outer)
    def _():
        pl.semaphore_wait(barrier, waits + 1)

    @pl.when(inner & (depth == 1))
    def _():
        pl.semaphore_wait(barrier, waits + 3)

    @pl.when(inner & (depth > 1))
    def _():
        pl.semaphore_wait(barrier, waits + 2)

    if square:
        for q in range(PARTS):
            for step in (1, 2):
                first_copy(step, q).start()
        for step in (1, 2):
            rest_copy(step).start()
    else:
        for step in range(1, n_blk):
            direct_copy(step).start()

    load_ratings.wait()

    def visit(step, carry):
        if square:
            for one in (1, 2):
                @pl.when(step == one)
                def _():
                    rest_copy(one).wait_recv()
        else:
            @pl.when(step > 0)
            def _():
                direct_copy(step).wait_recv()

        residues(step)
        user_terms(step, False)

        if square:
            @pl.when(step == 0)
            def _():
                for q in range(PARTS):
                    for one in (1, 2):
                        first_copy(one, q).wait_recv()
                        forward_copy(one, q).start()

        return carry

    final = n_blk - 1
    lax.fori_loop(0, final, visit, 0)
    direct_copy(final).wait_recv()
    residues(final)
    user_terms(final, True)

    def return_items(step, carry):
        terms = item_terms(step)

        @pl.when(step == 0)
        def _():
            item_own[...] = terms

        @pl.when(step > 0)
        def _():
            item_send[step] = encode(terms)
            item_copy(step).start()

        return carry

    lax.fori_loop(0, n_blk, return_items, 0)

    def hop(t, carry):
        @pl.when((t < high) & has_near)
        def _():
            arrived(0, t).wait_recv()
            total = user_sum[rows_of(t)] + decode(side_recv[0, t])
            side_send[0, t] = encode(total)

            far_copy(t).start()
            user_out[rows_of(t)] = total

        @pl.when(t >= low + lag)
        def _():
            c = t - lag
            mine = user_sum[rows_of(c)]

            arrived(1, c).wait_recv()
            beyond = decode(side_recv[1, c])

            @pl.when(has_near)
            def _():
                side_send[1, c] = encode(mine + beyond)
                near_copy(c).start()
                user_out[rows_of(c)] = (user_out[rows_of(c)] + beyond) * (1.0 / tile)

            @pl.when(outer)
            def _():
                user_out[rows_of(c)] = (mine + beyond) * (1.0 / tile)

            share_copy(c).start()

        return carry

    @pl.when(core == 1)
    def _():
        lax.fori_loop(low, chunks, fold, 0)

    @pl.when(outer | (core == 1))
    def _():
        lax.fori_loop(low, high + lag, hop, 0)

    returned = item_recv.at[pl.ds(1, n_blk - 1)]
    remote(
        returned, returned, send_sem.at[1], item_recv_sem.at[0], peer(1)
    ).wait_recv()

    def settle(step, carry):
        item_own[...] += decode(item_recv[step])
        return carry

    lax.fori_loop(1, n_blk, settle, 0)
    item_out[...] = item_own[...] * (1.0 / tile)

    def drain(ref, which):
        remote(ref, ref, send_sem.at[which], share_recv_sem.at[0], (blk, sibling)).wait_send()

    drain(panels.at[pl.ds(1, n_blk - 1)], 0)
    drain(item_send.at[pl.ds(1, n_blk - 1)], 1)

    def got(place):
        ref = pair_recv.at[place]
        remote(ref, ref, send_sem.at[5], share_recv_sem.at[0], (blk, sibling)).wait_recv()

    whole = pl.ds(0, chunks * CHUNK)
    first = pl.ds(0, early * CHUNK)
    second = pl.ds(early * CHUNK, (chunks - early) * CHUNK)

    @pl.when(has_near & (core == 0))
    def _():
        drain(pair_recv, 2)
        got(whole)

    @pl.when(outer & (core == 0))
    def _():
        drain(pair_recv.at[second], 2)
        drain(side_send.at[0, pl.ds(0, early)], 3)
        drain(pair_recv.at[first], 5)
        got(second)

    @pl.when(outer & (core == 1))
    def _():
        drain(pair_recv.at[first], 2)
        drain(side_send.at[0, pl.ds(early, chunks - early)], 3)
        drain(pair_recv.at[second], 5)
        got(first)

    @pl.when(inner)
    def _():
        drain(side_send.at[0], 3)
        drain(side_send.at[1], 4)
        drain(pair_recv, 5)


def settle_out(user_ref, item_ref, user_out, item_out, sem):
    copies = (
        pltpu.make_async_copy(user_ref, user_out, sem.at[0]),
        pltpu.make_async_copy(item_ref, item_out, sem.at[1]),
    )
    for copy in copies:
        copy.start()
    for copy in copies:
        copy.wait()


def body(user_factors, item_factors, ratings, tile_user, tile_item, tile_count):
    n_blk = lax.axis_size("blk")
    n_strata = lax.axis_size("strata")
    user_rows, rank = user_factors.shape
    panel_rows = item_factors.shape[0]
    slots, tile = ratings.shape[-3], ratings.shape[-1]
    user_tiles, panel_tiles = user_rows // tile, panel_rows // tile
    chunks = user_rows // CHUNK
    dma = pltpu.SemaphoreType.DMA
    counts = jnp.swapaxes(tile_count, 1, 2)
    operands = (
        user_factors.reshape(user_tiles, tile, rank),
        item_factors.reshape(panel_tiles, tile, rank),
        ratings,
        tile_user,
        tile_item,
        counts,
    )
    shapes = (
        jax.ShapeDtypeStruct((user_rows, rank), F32),
        jax.ShapeDtypeStruct((panel_rows, rank), F32),
    )
    grads = pl.pallas_call(
        functools.partial(kernel, n_blk, n_strata),
        out_shape=shapes,
        in_specs=[pl.BlockSpec(memory_space=pltpu.HBM)] * 6,
        out_specs=(
            pl.BlockSpec(memory_space=pltpu.VMEM),
            pl.BlockSpec(memory_space=pltpu.VMEM),
        ),
        scratch_shapes=[
            pltpu.SMEM(tile_user.shape, jnp.int32),
            pltpu.SMEM(tile_item.shape, jnp.int32),
            pltpu.SMEM(counts.shape, jnp.int32),
            pltpu.VMEM((user_tiles, tile, rank), BF16),
            pltpu.VMEM((n_blk, panel_tiles, tile, rank), BF16),
            pltpu.VMEM((panel_tiles, tile, rank), BF16),
            pltpu.VMEM((n_blk, slots, tile, tile), BF16),
            pltpu.VMEM((n_blk, slots * tile, rank), BF16),
            pltpu.VMEM((slots * tile, rank), BF16),
            pltpu.VMEM((n_blk, slots * tile, tile), BF16),
            pltpu.VMEM((user_rows, rank), F32),
            pltpu.VMEM((user_rows, rank), F32),
            pltpu.VMEM((2, chunks, CHUNK, rank), BF16),
            pltpu.VMEM((2, chunks, CHUNK, rank), BF16),
            pltpu.VMEM((panel_rows, rank), F32),
            pltpu.VMEM((n_blk, panel_rows, rank), BF16),
            pltpu.VMEM((n_blk, panel_rows, rank), BF16),
            dma((6,)),
            dma((2 * PARTS + 3 if n_blk == 4 else n_blk,)),
            dma((1,)),
            dma((user_tiles,)),
            dma((2, chunks)),
            dma((1,)),
            dma((6,)),
        ],
        compiler_params=pltpu.CompilerParams(
            collective_id=0, has_side_effects=True, vmem_limit_bytes=48 << 20
        ),
    )(*(pltpu.with_memory_space_constraint(x, pltpu.HBM) for x in operands))
    return pl.pallas_call(
        settle_out,
        out_shape=shapes,
        in_specs=[pl.BlockSpec(memory_space=pl.ANY)] * 2,
        out_specs=(pl.BlockSpec(memory_space=pltpu.HBM),) * 2,
        scratch_shapes=[dma((2,))],
        compiler_params=pltpu.CompilerParams(vmem_limit_bytes=1 << 20),
        cost_estimate=pl.CostEstimate(
            flops=0, bytes_accessed=8 * (user_rows + panel_rows) * rank, transcendentals=0
        ),
    )(*grads)


def solution(mesh):
    in_specs = (
        P("blk", None),
        P(("blk", "strata"), None),
        P("blk", None, "strata", None, None, None),
        P("blk", None, "strata", None),
        P("blk", None, "strata", None),
        P("blk", None, "strata"),
    )
    out_specs = (P("blk", None), P(("blk", "strata"), None))
    return jax.shard_map(body, mesh=mesh, in_specs=in_specs, out_specs=out_specs, check_vma=False)
```

```python
import functools

import jax
import jax.numpy as jnp
from jax import lax
from jax.experimental import pallas as pl
from jax.experimental.pallas import tpu as pltpu
from jax.sharding import PartitionSpec as P

MESH = pl.DeviceIdType.MESH
F32 = jnp.float32
BF16 = jnp.bfloat16
CHUNK = 32
LAG = 16
STEP_LAG = 28
PARTS = 2


def flip(place, step, size):
    other, bit = 0, 1
    while bit < size:
        other = other + bit * ((place // bit + step // bit) % 2)
        bit *= 2
    return other


def encode(x):
    return (x * jnp.abs(x) * (x * x)).astype(BF16)


def decode(code):
    y = code.astype(F32)
    size = jnp.maximum(jnp.abs(y), 1e-37)
    root = lax.rsqrt(size)
    return y * root * lax.rsqrt(size * root)


def kernel(
    n_blk,
    n_strata,
    users_hbm,
    items_hbm,
    ratings_hbm,
    rows_hbm,
    cols_hbm,
    count_hbm,
    user_out,
    item_out,
    rows_ref,
    cols_ref,
    count_ref,
    user_table,
    panels,
    panel_table,
    ratings,
    picked_users,
    picked_items,
    residue,
    user_sum,
    pair_recv,
    side_send,
    side_recv,
    item_own,
    item_send,
    item_recv,
    load_sem,
    gather_recv,
    item_recv_sem,
    pair_recv_sem,
    side_recv_sem,
    share_recv_sem,
    send_sem,
):
    user_tiles, tile, rank = user_table.shape
    panel_tiles = panels.shape[1]
    panel_rows = panel_tiles * tile
    slots = ratings.shape[1]
    chunks = side_send.shape[1]
    per_tile = tile // CHUNK
    blk = lax.axis_index("blk")
    strata = lax.axis_index("strata")
    core = strata % 2
    sibling = strata + 1 - 2 * core
    chip = strata // 2
    chips = n_strata // 2
    half = chips // 2
    upper = chip // half
    sign = 1 - 2 * upper
    far = (chip + sign) * 2 + 1
    depth = chip + upper * (chips - 1 - 2 * chip)
    has_near = depth > 0
    inner = has_near & (core == 1)
    outer = depth == 0
    early_tiles = user_tiles // 4
    early = early_tiles * per_tile
    inner0 = (has_near & (core == 0)) | (outer & (core == 1))
    low = (1 - has_near.astype(jnp.int32)) * core * early
    high = core * chunks + (1 - core) * (1 - has_near.astype(jnp.int32)) * early
    lag = LAG + STEP_LAG * (half - 1 - depth)
    crossing = depth // (half - 1) if half > 1 else depth + 1
    square = n_blk == 4
    greeted = (1, 2) if square else tuple(range(1, n_blk))

    def near(c):
        kept = (depth == 1) & (c < early)
        return (chip - sign) * 2 + 1 - kept.astype(jnp.int32)

    loads = [
        pltpu.make_async_copy(rows_hbm, rows_ref, load_sem.at[0]),
        pltpu.make_async_copy(cols_hbm, cols_ref, load_sem.at[1]),
        pltpu.make_async_copy(count_hbm, count_ref, load_sem.at[2]),
        pltpu.make_async_copy(items_hbm, panels.at[0], load_sem.at[3]),
        pltpu.make_async_copy(users_hbm, user_table, load_sem.at[4]),
    ]

    barrier = pltpu.get_barrier_semaphore()
    for step in greeted:
        pl.semaphore_signal(
            barrier, 1, device_id=(flip(blk, step, n_blk), strata), device_id_type=MESH
        )

    @pl.when(outer | (core == 1))
    def _():
        pl.semaphore_signal(barrier, 1, device_id=(blk, far), device_id_type=MESH)

    @pl.when(inner)
    def _():
        pl.semaphore_signal(barrier, 1, device_id=(blk, near(chunks)), device_id_type=MESH)

    @pl.when(inner & (depth == 1))
    def _():
        pl.semaphore_signal(barrier, 1, device_id=(blk, near(0)), device_id_type=MESH)

    pl.semaphore_signal(barrier, 1, device_id=(blk, sibling), device_id_type=MESH)

    for load in loads:
        load.start()

    load_ratings = pltpu.make_async_copy(
        ratings_hbm.at[0, pl.ds(0, n_blk), 0], ratings, load_sem.at[5]
    )
    load_ratings.start()

    def remote(src, dst, send, recv, device):
        return pltpu.make_async_remote_copy(
            src_ref=src,
            dst_ref=dst,
            send_sem=send,
            recv_sem=recv,
            device_id=device,
            device_id_type=MESH,
        )

    def peer(step):
        return (flip(blk, step, n_blk), strata)

    part = tile // PARTS

    def direct_copy(step):
        return remote(
            panels.at[0], panels.at[step],
            send_sem.at[0], gather_recv.at[2 * PARTS + 2 if square else step], peer(step),
        )

    def first_copy(step, q):
        place = (step - 1, pl.ds(q * part, part))
        return remote(
            panels.at[(0,) + place], panels.at[(step,) + place],
            send_sem.at[0], gather_recv.at[(step - 1) * PARTS + q], peer(step),
        )

    def rest_copy(step):
        return remote(
            panels.at[0, 2 - step], panels.at[step, 2 - step],
            send_sem.at[0], gather_recv.at[2 * PARTS + step - 1], peer(step),
        )

    def forward_copy(step, q):
        place = (step - 1, pl.ds(q * part, part))
        return remote(
            panels.at[(step,) + place], panels.at[(3,) + place],
            send_sem.at[0], gather_recv.at[2 * PARTS + 2],
            peer(3 - step),
        )

    def item_copy(step):
        return remote(
            item_send.at[step], item_recv.at[step],
            send_sem.at[1], item_recv_sem.at[0], peer(step),
        )

    def pair_copy(u):
        place = pl.ds(u * tile, tile)
        return remote(
            user_sum.at[place], pair_recv.at[place],
            send_sem.at[2], pair_recv_sem.at[u], (blk, sibling),
        )

    def far_copy(c):
        return remote(
            side_send.at[0, c], side_recv.at[crossing, c],
            send_sem.at[3], side_recv_sem.at[crossing, c], (blk, far),
        )

    def near_copy(c):
        return remote(
            side_send.at[1, c], side_recv.at[1, c],
            send_sem.at[4], side_recv_sem.at[1, c], (blk, near(c)),
        )

    def arrived(side, c):
        return remote(
            side_send.at[0, c], side_recv.at[side, c],
            send_sem.at[3], side_recv_sem.at[side, c], (blk, far),
        )

    def rows_of(c):
        return pl.ds(c * CHUNK, CHUNK)

    def share_copy(c):
        return remote(
            user_out.at[rows_of(c)], user_out.at[rows_of(c)],
            send_sem.at[5], share_recv_sem.at[0], (blk, sibling),
        )

    user_sum[...] = jnp.zeros(user_sum.shape, F32)

    def residues(step):
        source = flip(blk, step, n_blk)
        cols = [cols_ref[0, source, 0, k] for k in range(slots)]
        panel_table[...] = panels[step]
        for k in range(slots):
            place = slice(k * tile, (k + 1) * tile)
            picked_users[step, place] = user_table[rows_ref[0, source, 0, k]]
            picked_items[place] = panel_table[cols[k]]
        predicted = lax.dot_general(
            picked_users[step],
            panels[step].reshape(panel_rows, rank),
            (((1,), (1,)), ((), ())),
            preferred_element_type=F32,
        )
        for k in range(slots):
            place = slice(k * tile, (k + 1) * tile)
            live = (k < count_ref[0, 0, source]).astype(F32)
            chosen = predicted[place, :tile]
            for p in range(1, panel_tiles):
                chosen = jnp.where(cols[k] == p, predicted[place, p * tile : (p + 1) * tile], chosen)
            residue[step, place] = (
                (chosen - ratings[source, k].astype(F32)) * live
            ).astype(BF16)

    def hot(index, place):
        return jnp.full((tile, tile), (index == place).astype(F32), F32).astype(BF16)

    def fold(c, carry):
        @pl.when(c % per_tile == 0)
        def _():
            pair_copy(c // per_tile).wait_recv()

        mine = user_sum[rows_of(c)] + pair_recv[rows_of(c)]
        user_sum[rows_of(c)] = mine

        @pl.when(depth == 0)
        def _():
            side_send[0, c] = encode(mine)
            far_copy(c).start()

        return carry

    def user_terms(step, last):
        source = flip(blk, step, n_blk)
        for q in range(user_tiles // 2):
            rows = [
                jnp.concatenate(
                    [
                        residue[step, k * tile : (k + 1) * tile]
                        * hot(rows_ref[0, source, 0, k], 2 * q + one)
                        for k in range(slots)
                    ],
                    axis=1,
                )
                for one in range(2)
            ]
            place = slice(2 * q * tile, 2 * (q + 1) * tile)
            user_sum[place] += jnp.dot(
                jnp.concatenate(rows, axis=0), picked_items[...], preferred_element_type=F32
            )
            if last:
                for u in (2 * q, 2 * q + 1):
                    away = inner0 if u < early_tiles else core == 0

                    @pl.when(away)
                    def _():
                        pair_copy(u).start()

                if 2 * q < early_tiles:
                    @pl.when(outer & (core == 0))
                    def _():
                        lax.fori_loop(2 * q * per_tile, 2 * (q + 1) * per_tile, fold, 0)

    def item_terms(step):
        source = flip(blk, step, n_blk)
        by_item = jnp.concatenate(
            [
                jnp.concatenate(
                    [
                        residue[step, k * tile : (k + 1) * tile]
                        * hot(cols_ref[0, source, 0, k], p)
                        for p in range(panel_tiles)
                    ],
                    axis=1,
                )
                for k in range(slots)
            ],
            axis=0,
        )
        return lax.dot_general(
            by_item,
            picked_users[step],
            (((0,), (0,)), ((), ())),
            preferred_element_type=F32,
        )

    for load in loads:
        load.wait()

    waits = 1 + len(greeted)

    @pl.when(has_near & (core == 0))
    def _():
        pl.semaphore_wait(barrier, waits)

    @pl.when(outer)
    def _():
        pl.semaphore_wait(barrier, waits + 1)

    @pl.when(inner & (depth == 1))
    def _():
        pl.semaphore_wait(barrier, waits + 3)

    @pl.when(inner & (depth > 1))
    def _():
        pl.semaphore_wait(barrier, waits + 2)

    if square:
        for q in range(PARTS):
            for step in (1, 2):
                first_copy(step, q).start()
        for step in (1, 2):
            rest_copy(step).start()
    else:
        for step in range(1, n_blk):
            direct_copy(step).start()

    load_ratings.wait()

    def visit(step, carry):
        if square:
            for one in (1, 2):
                @pl.when(step == one)
                def _():
                    rest_copy(one).wait_recv()
        else:
            @pl.when(step > 0)
            def _():
                direct_copy(step).wait_recv()

        residues(step)
        user_terms(step, False)

        if square:
            @pl.when(step == 0)
            def _():
                for q in range(PARTS):
                    for one in (1, 2):
                        first_copy(one, q).wait_recv()
                        forward_copy(one, q).start()

        @pl.when(step == 0)
        def _():
            item_own[...] = item_terms(0)

        return carry

    final = n_blk - 1
    lax.fori_loop(0, final, visit, 0)
    direct_copy(final).wait_recv()
    residues(final)
    user_terms(final, True)

    def return_items(step, carry):
        item_send[step] = encode(item_terms(step))
        item_copy(step).start()
        return carry

    @pl.when(outer & (core == 1))
    def _():
        lax.fori_loop(low, chunks, fold, 0)

    lax.fori_loop(1, n_blk, return_items, 0)

    def hop(t, carry):
        @pl.when((t < high) & has_near)
        def _():
            arrived(0, t).wait_recv()
            total = user_sum[rows_of(t)] + decode(side_recv[0, t])
            side_send[0, t] = encode(total)

            far_copy(t).start()
            user_out[rows_of(t)] = total

        @pl.when(t >= low + lag)
        def _():
            c = t - lag
            mine = user_sum[rows_of(c)]

            arrived(1, c).wait_recv()
            beyond = decode(side_recv[1, c])

            @pl.when(has_near)
            def _():
                side_send[1, c] = encode(mine + beyond)
                near_copy(c).start()
                user_out[rows_of(c)] = (user_out[rows_of(c)] + beyond) * (1.0 / tile)

            @pl.when(outer)
            def _():
                user_out[rows_of(c)] = (mine + beyond) * (1.0 / tile)

            share_copy(c).start()

        return carry

    @pl.when(inner)
    def _():
        lax.fori_loop(low, chunks, fold, 0)

    @pl.when(outer | (core == 1))
    def _():
        lax.fori_loop(low, high + lag, hop, 0)

    returned = item_recv.at[pl.ds(1, n_blk - 1)]
    remote(
        returned, returned, send_sem.at[1], item_recv_sem.at[0], peer(1)
    ).wait_recv()

    def settle(step, carry):
        item_own[...] += decode(item_recv[step])
        return carry

    lax.fori_loop(1, n_blk, settle, 0)
    item_out[...] = item_own[...] * (1.0 / tile)

    def drain(ref, which):
        remote(ref, ref, send_sem.at[which], share_recv_sem.at[0], (blk, sibling)).wait_send()

    drain(panels.at[pl.ds(1, n_blk - 1)], 0)
    drain(item_send.at[pl.ds(1, n_blk - 1)], 1)

    def got(place):
        ref = pair_recv.at[place]
        remote(ref, ref, send_sem.at[5], share_recv_sem.at[0], (blk, sibling)).wait_recv()

    whole = pl.ds(0, chunks * CHUNK)
    first = pl.ds(0, early * CHUNK)
    second = pl.ds(early * CHUNK, (chunks - early) * CHUNK)

    @pl.when(has_near & (core == 0))
    def _():
        drain(pair_recv, 2)
        got(whole)

    @pl.when(outer & (core == 0))
    def _():
        drain(pair_recv.at[second], 2)
        drain(side_send.at[0, pl.ds(0, early)], 3)
        drain(pair_recv.at[first], 5)
        got(second)

    @pl.when(outer & (core == 1))
    def _():
        drain(pair_recv.at[first], 2)
        drain(side_send.at[0, pl.ds(early, chunks - early)], 3)
        drain(pair_recv.at[second], 5)
        got(first)

    @pl.when(inner)
    def _():
        drain(side_send.at[0], 3)
        drain(side_send.at[1], 4)
        drain(pair_recv, 5)


def settle_out(user_ref, item_ref, user_out, item_out, sem):
    copies = (
        pltpu.make_async_copy(user_ref, user_out, sem.at[0]),
        pltpu.make_async_copy(item_ref, item_out, sem.at[1]),
    )
    for copy in copies:
        copy.start()
    for copy in copies:
        copy.wait()


def body(user_factors, item_factors, ratings, tile_user, tile_item, tile_count):
    n_blk = lax.axis_size("blk")
    n_strata = lax.axis_size("strata")
    user_rows, rank = user_factors.shape
    panel_rows = item_factors.shape[0]
    slots, tile = ratings.shape[-3], ratings.shape[-1]
    user_tiles, panel_tiles = user_rows // tile, panel_rows // tile
    chunks = user_rows // CHUNK
    dma = pltpu.SemaphoreType.DMA
    counts = jnp.swapaxes(tile_count, 1, 2)
    operands = (
        user_factors.reshape(user_tiles, tile, rank),
        item_factors.reshape(panel_tiles, tile, rank),
        ratings,
        tile_user,
        tile_item,
        counts,
    )
    shapes = (
        jax.ShapeDtypeStruct((user_rows, rank), F32),
        jax.ShapeDtypeStruct((panel_rows, rank), F32),
    )
    grads = pl.pallas_call(
        functools.partial(kernel, n_blk, n_strata),
        out_shape=shapes,
        in_specs=[pl.BlockSpec(memory_space=pltpu.HBM)] * 6,
        out_specs=(
            pl.BlockSpec(memory_space=pltpu.VMEM),
            pl.BlockSpec(memory_space=pltpu.VMEM),
        ),
        scratch_shapes=[
            pltpu.SMEM(tile_user.shape, jnp.int32),
            pltpu.SMEM(tile_item.shape, jnp.int32),
            pltpu.SMEM(counts.shape, jnp.int32),
            pltpu.VMEM((user_tiles, tile, rank), BF16),
            pltpu.VMEM((n_blk, panel_tiles, tile, rank), BF16),
            pltpu.VMEM((panel_tiles, tile, rank), BF16),
            pltpu.VMEM((n_blk, slots, tile, tile), BF16),
            pltpu.VMEM((n_blk, slots * tile, rank), BF16),
            pltpu.VMEM((slots * tile, rank), BF16),
            pltpu.VMEM((n_blk, slots * tile, tile), BF16),
            pltpu.VMEM((user_rows, rank), F32),
            pltpu.VMEM((user_rows, rank), F32),
            pltpu.VMEM((2, chunks, CHUNK, rank), BF16),
            pltpu.VMEM((2, chunks, CHUNK, rank), BF16),
            pltpu.VMEM((panel_rows, rank), F32),
            pltpu.VMEM((n_blk, panel_rows, rank), BF16),
            pltpu.VMEM((n_blk, panel_rows, rank), BF16),
            dma((6,)),
            dma((2 * PARTS + 3 if n_blk == 4 else n_blk,)),
            dma((1,)),
            dma((user_tiles,)),
            dma((2, chunks)),
            dma((1,)),
            dma((6,)),
        ],
        compiler_params=pltpu.CompilerParams(
            collective_id=0, has_side_effects=True, vmem_limit_bytes=48 << 20
        ),
    )(*(pltpu.with_memory_space_constraint(x, pltpu.HBM) for x in operands))
    return pl.pallas_call(
        settle_out,
        out_shape=shapes,
        in_specs=[pl.BlockSpec(memory_space=pl.ANY)] * 2,
        out_specs=(pl.BlockSpec(memory_space=pltpu.HBM),) * 2,
        scratch_shapes=[dma((2,))],
        compiler_params=pltpu.CompilerParams(vmem_limit_bytes=1 << 20),
        cost_estimate=pl.CostEstimate(
            flops=0, bytes_accessed=8 * (user_rows + panel_rows) * rank, transcendentals=0
        ),
    )(*grads)


def solution(mesh):
    in_specs = (
        P("blk", None),
        P(("blk", "strata"), None),
        P("blk", None, "strata", None, None, None),
        P("blk", None, "strata", None),
        P("blk", None, "strata", None),
        P("blk", None, "strata"),
    )
    out_specs = (P("blk", None), P(("blk", "strata"), None))
    return jax.shard_map(body, mesh=mesh, in_specs=in_specs, out_specs=out_specs, check_vma=False)
```

```python
import functools

import jax
import jax.numpy as jnp
from jax import lax
from jax.experimental import pallas as pl
from jax.experimental.pallas import tpu as pltpu
from jax.sharding import PartitionSpec as P

MESH = pl.DeviceIdType.MESH
F32 = jnp.float32
BF16 = jnp.bfloat16
CHUNK = 32
LAG = 16
STEP_LAG = 28
PARTS = 2


def flip(place, step, size):
    other, bit = 0, 1
    while bit < size:
        other = other + bit * ((place // bit + step // bit) % 2)
        bit *= 2
    return other


def encode(x):
    return (x * jnp.abs(x) * (x * x)).astype(BF16)


def decode(code):
    y = code.astype(F32)
    size = jnp.maximum(jnp.abs(y), 1e-37)
    root = lax.rsqrt(size)
    return y * root * lax.rsqrt(size * root)


def kernel(
    n_blk,
    n_strata,
    users_hbm,
    items_hbm,
    ratings_hbm,
    rows_hbm,
    cols_hbm,
    count_hbm,
    user_out,
    item_out,
    rows_ref,
    cols_ref,
    count_ref,
    user_table,
    panels,
    panel_table,
    ratings,
    picked_users,
    picked_items,
    residue,
    user_sum,
    pair_recv,
    side_send,
    side_recv,
    item_own,
    item_send,
    item_recv,
    load_sem,
    gather_recv,
    item_recv_sem,
    pair_recv_sem,
    side_recv_sem,
    share_recv_sem,
    send_sem,
):
    user_tiles, tile, rank = user_table.shape
    panel_tiles = panels.shape[1]
    panel_rows = panel_tiles * tile
    slots = ratings.shape[1]
    chunks = side_send.shape[1]
    per_tile = tile // CHUNK
    blk = lax.axis_index("blk")
    strata = lax.axis_index("strata")
    core = strata % 2
    sibling = strata + 1 - 2 * core
    chip = strata // 2
    chips = n_strata // 2
    half = chips // 2
    upper = chip // half
    sign = 1 - 2 * upper
    far = (chip + sign) * 2 + 1
    depth = chip + upper * (chips - 1 - 2 * chip)
    has_near = depth > 0
    inner = has_near & (core == 1)
    outer = depth == 0
    early_tiles = user_tiles // 8
    early = early_tiles * per_tile
    inner0 = (has_near & (core == 0)) | (outer & (core == 1))
    low = (1 - has_near.astype(jnp.int32)) * core * early
    high = core * chunks + (1 - core) * (1 - has_near.astype(jnp.int32)) * early
    lag = LAG + STEP_LAG * (half - 1 - depth)
    crossing = depth // (half - 1) if half > 1 else depth + 1
    square = n_blk == 4
    greeted = (1, 2) if square else tuple(range(1, n_blk))

    def near(c):
        kept = (depth == 1) & (c < early)
        return (chip - sign) * 2 + 1 - kept.astype(jnp.int32)

    loads = [
        pltpu.make_async_copy(rows_hbm, rows_ref, load_sem.at[0]),
        pltpu.make_async_copy(cols_hbm, cols_ref, load_sem.at[1]),
        pltpu.make_async_copy(count_hbm, count_ref, load_sem.at[2]),
        pltpu.make_async_copy(items_hbm, panels.at[0], load_sem.at[3]),
        pltpu.make_async_copy(users_hbm, user_table, load_sem.at[4]),
    ]

    barrier = pltpu.get_barrier_semaphore()
    for step in greeted:
        pl.semaphore_signal(
            barrier, 1, device_id=(flip(blk, step, n_blk), strata), device_id_type=MESH
        )

    @pl.when(outer | (core == 1))
    def _():
        pl.semaphore_signal(barrier, 1, device_id=(blk, far), device_id_type=MESH)

    @pl.when(inner)
    def _():
        pl.semaphore_signal(barrier, 1, device_id=(blk, near(chunks)), device_id_type=MESH)

    @pl.when(inner & (depth == 1))
    def _():
        pl.semaphore_signal(barrier, 1, device_id=(blk, near(0)), device_id_type=MESH)

    pl.semaphore_signal(barrier, 1, device_id=(blk, sibling), device_id_type=MESH)

    for load in loads:
        load.start()

    load_ratings = pltpu.make_async_copy(
        ratings_hbm.at[0, pl.ds(0, n_blk), 0], ratings, load_sem.at[5]
    )
    load_ratings.start()

    def remote(src, dst, send, recv, device):
        return pltpu.make_async_remote_copy(
            src_ref=src,
            dst_ref=dst,
            send_sem=send,
            recv_sem=recv,
            device_id=device,
            device_id_type=MESH,
        )

    def peer(step):
        return (flip(blk, step, n_blk), strata)

    part = tile // PARTS

    def direct_copy(step):
        return remote(
            panels.at[0], panels.at[step],
            send_sem.at[0], gather_recv.at[2 * PARTS + 2 if square else step], peer(step),
        )

    def first_copy(step, q):
        place = (step - 1, pl.ds(q * part, part))
        return remote(
            panels.at[(0,) + place], panels.at[(step,) + place],
            send_sem.at[0], gather_recv.at[(step - 1) * PARTS + q], peer(step),
        )

    def rest_copy(step):
        return remote(
            panels.at[0, 2 - step], panels.at[step, 2 - step],
            send_sem.at[0], gather_recv.at[2 * PARTS + step - 1], peer(step),
        )

    def forward_copy(step, q):
        place = (step - 1, pl.ds(q * part, part))
        return remote(
            panels.at[(step,) + place], panels.at[(3,) + place],
            send_sem.at[0], gather_recv.at[2 * PARTS + 2],
            peer(3 - step),
        )

    def item_copy(step):
        return remote(
            item_send.at[step], item_recv.at[step],
            send_sem.at[1], item_recv_sem.at[0], peer(step),
        )

    def pair_copy(u):
        place = pl.ds(u * tile, tile)
        return remote(
            user_sum.at[place], pair_recv.at[place],
            send_sem.at[2], pair_recv_sem.at[u], (blk, sibling),
        )

    def far_copy(c):
        return remote(
            side_send.at[0, c], side_recv.at[crossing, c],
            send_sem.at[3], side_recv_sem.at[crossing, c], (blk, far),
        )

    def near_copy(c):
        return remote(
            side_send.at[1, c], side_recv.at[1, c],
            send_sem.at[4], side_recv_sem.at[1, c], (blk, near(c)),
        )

    def arrived(side, c):
        return remote(
            side_send.at[0, c], side_recv.at[side, c],
            send_sem.at[3], side_recv_sem.at[side, c], (blk, far),
        )

    def rows_of(c):
        return pl.ds(c * CHUNK, CHUNK)

    def share_copy(c):
        return remote(
            user_out.at[rows_of(c)], user_out.at[rows_of(c)],
            send_sem.at[5], share_recv_sem.at[0], (blk, sibling),
        )

    user_sum[...] = jnp.zeros(user_sum.shape, F32)

    def residues(step):
        source = flip(blk, step, n_blk)
        cols = [cols_ref[0, source, 0, k] for k in range(slots)]
        panel_table[...] = panels[step]
        for k in range(slots):
            place = slice(k * tile, (k + 1) * tile)
            picked_users[step, place] = user_table[rows_ref[0, source, 0, k]]
            picked_items[place] = panel_table[cols[k]]
        predicted = lax.dot_general(
            picked_users[step],
            panels[step].reshape(panel_rows, rank),
            (((1,), (1,)), ((), ())),
            preferred_element_type=F32,
        )
        for k in range(slots):
            place = slice(k * tile, (k + 1) * tile)
            live = (k < count_ref[0, 0, source]).astype(F32)
            chosen = predicted[place, :tile]
            for p in range(1, panel_tiles):
                chosen = jnp.where(cols[k] == p, predicted[place, p * tile : (p + 1) * tile], chosen)
            residue[step, place] = (
                (chosen - ratings[source, k].astype(F32)) * live
            ).astype(BF16)

    def hot(index, place):
        return jnp.full((tile, tile), (index == place).astype(F32), F32).astype(BF16)

    def fold(c, carry):
        @pl.when(c % per_tile == 0)
        def _():
            pair_copy(c // per_tile).wait_recv()

        mine = user_sum[rows_of(c)] + pair_recv[rows_of(c)]
        user_sum[rows_of(c)] = mine

        @pl.when(depth == 0)
        def _():
            side_send[0, c] = encode(mine)
            far_copy(c).start()

        return carry

    def user_terms(step, last):
        source = flip(blk, step, n_blk)
        for q in range(user_tiles // 2):
            rows = [
                jnp.concatenate(
                    [
                        residue[step, k * tile : (k + 1) * tile]
                        * hot(rows_ref[0, source, 0, k], 2 * q + one)
                        for k in range(slots)
                    ],
                    axis=1,
                )
                for one in range(2)
            ]
            place = slice(2 * q * tile, 2 * (q + 1) * tile)
            user_sum[place] += jnp.dot(
                jnp.concatenate(rows, axis=0), picked_items[...], preferred_element_type=F32
            )
            if last:
                for u in (2 * q, 2 * q + 1):
                    away = inner0 if u < early_tiles else core == 0

                    @pl.when(away)
                    def _():
                        pair_copy(u).start()

                if 2 * q < early_tiles:
                    @pl.when(outer & (core == 0))
                    def _():
                        lax.fori_loop(
                            2 * q * per_tile, min(2 * (q + 1) * per_tile, early), fold, 0
                        )

    def item_terms(step):
        source = flip(blk, step, n_blk)
        by_item = jnp.concatenate(
            [
                jnp.concatenate(
                    [
                        residue[step, k * tile : (k + 1) * tile]
                        * hot(cols_ref[0, source, 0, k], p)
                        for p in range(panel_tiles)
                    ],
                    axis=1,
                )
                for k in range(slots)
            ],
            axis=0,
        )
        return lax.dot_general(
            by_item,
            picked_users[step],
            (((0,), (0,)), ((), ())),
            preferred_element_type=F32,
        )

    for load in loads:
        load.wait()

    waits = 1 + len(greeted)

    @pl.when(has_near & (core == 0))
    def _():
        pl.semaphore_wait(barrier, waits)

    @pl.when(outer)
    def _():
        pl.semaphore_wait(barrier, waits + 1)

    @pl.when(inner & (depth == 1))
    def _():
        pl.semaphore_wait(barrier, waits + 3)

    @pl.when(inner & (depth > 1))
    def _():
        pl.semaphore_wait(barrier, waits + 2)

    if square:
        for q in range(PARTS):
            for step in (1, 2):
                first_copy(step, q).start()
        for step in (1, 2):
            rest_copy(step).start()
    else:
        for step in range(1, n_blk):
            direct_copy(step).start()

    load_ratings.wait()

    def visit(step, carry):
        if square:
            for one in (1, 2):
                @pl.when(step == one)
                def _():
                    rest_copy(one).wait_recv()
        else:
            @pl.when(step > 0)
            def _():
                direct_copy(step).wait_recv()

        residues(step)
        user_terms(step, False)

        if square:
            @pl.when(step == 0)
            def _():
                for q in range(PARTS):
                    for one in (1, 2):
                        first_copy(one, q).wait_recv()
                        forward_copy(one, q).start()

        @pl.when(step == 0)
        def _():
            item_own[...] = item_terms(0)

        return carry

    final = n_blk - 1
    lax.fori_loop(0, final, visit, 0)
    direct_copy(final).wait_recv()
    residues(final)
    user_terms(final, True)

    def return_items(step, carry):
        item_send[step] = encode(item_terms(step))
        item_copy(step).start()
        return carry

    @pl.when(outer & (core == 1))
    def _():
        lax.fori_loop(low, chunks, fold, 0)

    lax.fori_loop(1, n_blk, return_items, 0)

    def hop(t, carry):
        @pl.when((t < high) & has_near)
        def _():
            arrived(0, t).wait_recv()
            total = user_sum[rows_of(t)] + decode(side_recv[0, t])
            side_send[0, t] = encode(total)

            far_copy(t).start()
            user_out[rows_of(t)] = total

        @pl.when(t >= low + lag)
        def _():
            c = t - lag
            mine = user_sum[rows_of(c)]

            arrived(1, c).wait_recv()
            beyond = decode(side_recv[1, c])

            @pl.when(has_near)
            def _():
                side_send[1, c] = encode(mine + beyond)
                near_copy(c).start()
                user_out[rows_of(c)] = (user_out[rows_of(c)] + beyond) * (1.0 / tile)

            @pl.when(outer)
            def _():
                user_out[rows_of(c)] = (mine + beyond) * (1.0 / tile)

            share_copy(c).start()

        return carry

    @pl.when(inner)
    def _():
        lax.fori_loop(low, chunks, fold, 0)

    @pl.when(outer | (core == 1))
    def _():
        lax.fori_loop(low, high + lag, hop, 0)

    returned = item_recv.at[pl.ds(1, n_blk - 1)]
    remote(
        returned, returned, send_sem.at[1], item_recv_sem.at[0], peer(1)
    ).wait_recv()

    def settle(step, carry):
        item_own[...] += decode(item_recv[step])
        return carry

    lax.fori_loop(1, n_blk, settle, 0)
    item_out[...] = item_own[...] * (1.0 / tile)

    def drain(ref, which):
        remote(ref, ref, send_sem.at[which], share_recv_sem.at[0], (blk, sibling)).wait_send()

    drain(panels.at[pl.ds(1, n_blk - 1)], 0)
    drain(item_send.at[pl.ds(1, n_blk - 1)], 1)

    def got(place):
        ref = pair_recv.at[place]
        remote(ref, ref, send_sem.at[5], share_recv_sem.at[0], (blk, sibling)).wait_recv()

    whole = pl.ds(0, chunks * CHUNK)
    first = pl.ds(0, early * CHUNK)
    second = pl.ds(early * CHUNK, (chunks - early) * CHUNK)

    @pl.when(has_near & (core == 0))
    def _():
        drain(pair_recv, 2)
        got(whole)

    @pl.when(outer & (core == 0))
    def _():
        drain(pair_recv.at[second], 2)
        drain(side_send.at[0, pl.ds(0, early)], 3)
        drain(pair_recv.at[first], 5)
        got(second)

    @pl.when(outer & (core == 1))
    def _():
        drain(pair_recv.at[first], 2)
        drain(side_send.at[0, pl.ds(early, chunks - early)], 3)
        drain(pair_recv.at[second], 5)
        got(first)

    @pl.when(inner)
    def _():
        drain(side_send.at[0], 3)
        drain(side_send.at[1], 4)
        drain(pair_recv, 5)


def settle_out(user_ref, item_ref, user_out, item_out, sem):
    copies = (
        pltpu.make_async_copy(user_ref, user_out, sem.at[0]),
        pltpu.make_async_copy(item_ref, item_out, sem.at[1]),
    )
    for copy in copies:
        copy.start()
    for copy in copies:
        copy.wait()


def body(user_factors, item_factors, ratings, tile_user, tile_item, tile_count):
    n_blk = lax.axis_size("blk")
    n_strata = lax.axis_size("strata")
    user_rows, rank = user_factors.shape
    panel_rows = item_factors.shape[0]
    slots, tile = ratings.shape[-3], ratings.shape[-1]
    user_tiles, panel_tiles = user_rows // tile, panel_rows // tile
    chunks = user_rows // CHUNK
    dma = pltpu.SemaphoreType.DMA
    counts = jnp.swapaxes(tile_count, 1, 2)
    operands = (
        user_factors.reshape(user_tiles, tile, rank),
        item_factors.reshape(panel_tiles, tile, rank),
        ratings,
        tile_user,
        tile_item,
        counts,
    )
    shapes = (
        jax.ShapeDtypeStruct((user_rows, rank), F32),
        jax.ShapeDtypeStruct((panel_rows, rank), F32),
    )
    grads = pl.pallas_call(
        functools.partial(kernel, n_blk, n_strata),
        out_shape=shapes,
        in_specs=[pl.BlockSpec(memory_space=pltpu.HBM)] * 6,
        out_specs=(
            pl.BlockSpec(memory_space=pltpu.VMEM),
            pl.BlockSpec(memory_space=pltpu.VMEM),
        ),
        scratch_shapes=[
            pltpu.SMEM(tile_user.shape, jnp.int32),
            pltpu.SMEM(tile_item.shape, jnp.int32),
            pltpu.SMEM(counts.shape, jnp.int32),
            pltpu.VMEM((user_tiles, tile, rank), BF16),
            pltpu.VMEM((n_blk, panel_tiles, tile, rank), BF16),
            pltpu.VMEM((panel_tiles, tile, rank), BF16),
            pltpu.VMEM((n_blk, slots, tile, tile), BF16),
            pltpu.VMEM((n_blk, slots * tile, rank), BF16),
            pltpu.VMEM((slots * tile, rank), BF16),
            pltpu.VMEM((n_blk, slots * tile, tile), BF16),
            pltpu.VMEM((user_rows, rank), F32),
            pltpu.VMEM((user_rows, rank), F32),
            pltpu.VMEM((2, chunks, CHUNK, rank), BF16),
            pltpu.VMEM((2, chunks, CHUNK, rank), BF16),
            pltpu.VMEM((panel_rows, rank), F32),
            pltpu.VMEM((n_blk, panel_rows, rank), BF16),
            pltpu.VMEM((n_blk, panel_rows, rank), BF16),
            dma((6,)),
            dma((2 * PARTS + 3 if n_blk == 4 else n_blk,)),
            dma((1,)),
            dma((user_tiles,)),
            dma((2, chunks)),
            dma((1,)),
            dma((6,)),
        ],
        compiler_params=pltpu.CompilerParams(
            collective_id=0, has_side_effects=True, vmem_limit_bytes=48 << 20
        ),
    )(*(pltpu.with_memory_space_constraint(x, pltpu.HBM) for x in operands))
    return pl.pallas_call(
        settle_out,
        out_shape=shapes,
        in_specs=[pl.BlockSpec(memory_space=pl.ANY)] * 2,
        out_specs=(pl.BlockSpec(memory_space=pltpu.HBM),) * 2,
        scratch_shapes=[dma((2,))],
        compiler_params=pltpu.CompilerParams(vmem_limit_bytes=1 << 20),
        cost_estimate=pl.CostEstimate(
            flops=0, bytes_accessed=8 * (user_rows + panel_rows) * rank, transcendentals=0
        ),
    )(*grads)


def solution(mesh):
    in_specs = (
        P("blk", None),
        P(("blk", "strata"), None),
        P("blk", None, "strata", None, None, None),
        P("blk", None, "strata", None),
        P("blk", None, "strata", None),
        P("blk", None, "strata"),
    )
    out_specs = (P("blk", None), P(("blk", "strata"), None))
    return jax.shard_map(body, mesh=mesh, in_specs=in_specs, out_specs=out_specs, check_vma=False)
```
